1024 devices in a mesh: gx: 32 (over z), gy: 8 (over y, core), gz: 4 (over x).
Axes of the slice: x: 4, y: 4, z: 32, core: 2. Of those that a mesh axis runs over, the one named last changes fastest.
Arguments:
- compliance: float32 [32, 8, 4, 768, 768], P('gx', 'gy', 'gz'), may hold values from -1 to 3, as said below
- rigid_modes: float32 [32, 8, 4, 6, 3, 2, 128], P('gx', 'gy', 'gz'), may hold values from -0.21875 to 0.21875
- coarse_inverse: float32 [6144, 6144], P(('gx', 'gy', 'gz')), may hold values from -1 to 1, as said below
- coarse_rhs: float32 [32, 8, 4, 6, 64], P('gx', 'gy', 'gz'), may hold values from -48 to 48
- dual_rhs: float32 [32, 8, 4, 3, 2, 64, 128], P('gx', 'gy', 'gz'), may hold values from -100 to 100, as said below
Outputs:
- multipliers: float32 [32, 8, 4, 3, 2, 64, 128], P('gx', 'gy', 'gz')
- final_residual: float32 [32, 8, 4, 3, 2, 64, 128], P('gx', 'gy', 'gz')
The draws below stay inside these ranges and needn't reach their ends.
Inputs may be any that keep to these rules, and one draw needn't show every extreme that they name: Each subdomain's compliance block is symmetric positive definite. `coarse_inverse`: symmetric. `dual_rhs`: on every subdomain, the minus side of a direction holds the negated plus side of the previous subdomain in that direction, and zeros where there is none.
All inputs are finite; a program needn't handle non-finite values.
Results may differ from the reference program's by a relative error of at most 0.0023.
The reference program's roundings to bfloat16 on the way count: a program that leaves them out, or rounds other values in their place, can miss the bound.
Values may be sent and summed in bfloat16 or wider, within the bound.
No kernel may reach another device: no remote copies, remote signals or barrier semaphores. Data moves between devices by JAX's collectives and lax.ppermute only.
A program may use at most 32 MiB of HBM per device.

```python
import math
import jax
import jax.numpy as jnp
from jax import lax

FACE = 128
MODES = 6
LOADS = 64
ITERS = 1
SX = 32
SY = 8
SZ = 4
COARSE = 6144


def draw_compliance(key, part):
    order_size = 6 * FACE
    subdomains = SX * SY * SZ

    def one_block(block_key):
        noise_key, diag_key = jax.random.split(block_key)
        noise_draw = jnp.clip(jax.random.normal(noise_key, (order_size, order_size), jnp.float32), -5.0, 5.0)
        symmetric = (noise_draw + noise_draw.T) / math.sqrt(2.0)
        diagonal = jax.random.uniform(diag_key, (order_size,), jnp.float32, 1.2, 2.0)
        return jnp.diag(diagonal) + 0.5 * symmetric / math.sqrt(order_size)
    blocks = lax.map(one_block, jax.random.split(key, subdomains))
    return blocks.reshape(SX, SY, SZ, order_size, order_size)


def draw_coarse_inverse(key, part):
    coarse_size = COARSE
    noise_draw = jnp.clip(jax.random.normal(key, (coarse_size, coarse_size), jnp.float32), -5.0, 5.0)
    symmetric = (noise_draw + noise_draw.T) / math.sqrt(2.0)
    return 0.5 * (jnp.eye(coarse_size, dtype=jnp.float32) + 0.5 * symmetric / math.sqrt(coarse_size))


def from_lower_drawn(values, axis):
    length = values.shape[axis]
    zero_rim = jnp.zeros_like(lax.slice_in_dim(values, 0, 1, axis=axis))
    return jnp.concatenate([zero_rim, lax.slice_in_dim(values, 0, length - 1, axis=axis)], axis=axis)


def draw_dual_rhs(key, part):
    key_list = jax.random.split(key, 3)
    shape_full = (SX, SY, SZ, 3, LOADS, FACE)
    base_draw = jnp.clip(jax.random.normal(key_list[0], shape_full, jnp.float32), -4.0, 4.0)
    divisor = 12.0
    load_scale = jnp.exp(jax.random.uniform(key_list[1], (LOADS, 1), jnp.float32, 0.0, math.log(10.0)))
    unknown_scale = jnp.exp(jax.random.uniform(key_list[2], (SX, SY, SZ, 3, 1, FACE), jnp.float32, 0.0, math.log(10.0)))
    rising = 0.5 + (jnp.arange(SX, dtype=jnp.float32) + 0.5) / SX
    rising = rising.reshape(SX, 1, 1, 1, 1, 1)
    plus_faces = base_draw * load_scale * unknown_scale * rising / divisor
    shifted = [from_lower_drawn(plus_faces[:, :, :, direction], direction) for direction in range(3)]
    minus_faces = -jnp.stack(shifted, axis=3)
    return jnp.stack([minus_faces, plus_faces], axis=4)


def block_scale(rng, extent, pieces, least, largest):
    loudness, own = 1.0, jax.random.fold_in(rng, 6)
    for position, shards_of in pieces:
        heights = jnp.exp(jax.random.uniform(jax.random.fold_in(own, position), (shards_of,), jnp.float32, least / len(pieces), largest / len(pieces)))
        loudness = loudness * jnp.repeat(heights, extent[position] // shards_of).reshape([-1 if axis == position else 1 for axis in range(len(extent))])
    return loudness


def bell_draw(stream_key, extent, deviation, limit, cuts=(), kind=jnp.bfloat16):
    array = deviation * jax.random.normal(stream_key, extent, jnp.float32)
    if cuts:
        array = array * block_scale(stream_key, extent, cuts, -0.22, 0.18)
    return jnp.clip(array, -limit, limit).astype(kind)


def setup_inputs(seed: int = 0) -> dict:
    keys = jax.random.split(jax.random.key(seed), 6)
    compliance = draw_compliance(jax.random.fold_in(keys[5], 71), 0)
    rigid_modes = bell_draw(keys[1], (SX, SY, SZ, MODES, 3, 2, FACE), (6 * FACE) ** -0.5, 0.21875, ((0, 32), (1, 8), (2, 4)), jnp.float32)
    coarse_inverse = draw_coarse_inverse(jax.random.fold_in(keys[5], 71), 0)
    coarse_rhs = bell_draw(keys[3], (SX, SY, SZ, MODES, LOADS), 8.0, 48.0, ((0, 32), (1, 8), (2, 4)), jnp.float32)
    dual_rhs = draw_dual_rhs(jax.random.fold_in(keys[5], 71), 0)
    return {"compliance": compliance, "rigid_modes": rigid_modes, "coarse_inverse": coarse_inverse, "coarse_rhs": coarse_rhs, "dual_rhs": dual_rhs}


HIGHEST = lax.Precision.HIGHEST

def from_lower(values, axis):
    length = values.shape[axis]
    zero_rim = jnp.zeros_like(lax.slice_in_dim(values, 0, 1, axis=axis))
    return jnp.concatenate([zero_rim, lax.slice_in_dim(values, 0, length - 1, axis=axis)], axis=axis)

def from_upper(values, axis):
    length = values.shape[axis]
    zero_rim = jnp.zeros_like(lax.slice_in_dim(values, 0, 1, axis=axis))
    return jnp.concatenate([lax.slice_in_dim(values, 1, length, axis=axis), zero_rim], axis=axis)

def assemble(values):
    blocks = []
    for direction in range(3):
        minus_side = values[:, :, :, direction, 0]
        plus_side = values[:, :, :, direction, 1]
        new_plus = plus_side - from_upper(minus_side, direction)
        new_minus = minus_side - from_lower(plus_side, direction)
        inside = lax.broadcasted_iota(jnp.int32, new_minus.shape, direction) > 0
        new_minus = jnp.where(inside, new_minus, jnp.zeros_like(new_minus))
        blocks.append(jnp.stack([new_minus, new_plus], axis=3))
    return jnp.stack(blocks, axis=3)

def comply(compliance, values):
    matrix = compliance.reshape(SX, SY, SZ, 3, 2, FACE, 3, 2, FACE)
    return jnp.einsum('abcijdklm,abcklnm->abcijnd', matrix, values, precision=HIGHEST)

def coarse(rigid_modes, coarse_inverse, right_side):
    stacked = right_side.reshape(COARSE, LOADS).astype(jnp.bfloat16)
    stacked = lax.optimization_barrier(stacked).astype(jnp.float32)
    weights = jnp.dot(coarse_inverse, stacked, precision=HIGHEST).reshape(SX, SY, SZ, MODES, LOADS)
    correction = jnp.einsum('abcmijd,abcmn->abcijnd', rigid_modes, weights, precision=HIGHEST)
    return assemble(correction)

def project(rigid_modes, coarse_inverse, residual):
    right_side = jnp.einsum('abcmijd,abcijnd->abcmn', rigid_modes, residual, precision=HIGHEST)
    return residual - coarse(rigid_modes, coarse_inverse, right_side)

def inner_block(first_field, second_field):
    return jnp.einsum('abcind,abcimd->nm', first_field[:, :, :, :, 1], second_field[:, :, :, :, 1], precision=HIGHEST)

def gram_solve(matrix, target):
    factor = jnp.linalg.cholesky(matrix)
    middle = lax.linalg.triangular_solve(factor, target, left_side=True, lower=True)
    return lax.linalg.triangular_solve(factor, middle, left_side=True, lower=True, transpose_a=True)

def combine(values, coeffs):
    return jnp.einsum('abcijnd,nm->abcijmd', values, coeffs, precision=HIGHEST)

def reference(compliance, rigid_modes, coarse_inverse, coarse_rhs, dual_rhs):
    multipliers = coarse(rigid_modes, coarse_inverse, coarse_rhs)
    residual = dual_rhs - assemble(comply(compliance, multipliers))
    projected = project(rigid_modes, coarse_inverse, residual)
    direction = projected
    for number in range(ITERS):
        applied = assemble(comply(compliance, direction))
        curvature = inner_block(direction, applied)
        step_size = gram_solve(curvature, inner_block(direction, projected))
        multipliers = multipliers + combine(direction, step_size)
        if number + 1 < ITERS:
            residual = residual - combine(applied, step_size)
            projected = project(rigid_modes, coarse_inverse, residual)
            correction = -gram_solve(curvature, inner_block(applied, projected))
            direction = projected + combine(direction, correction)
    final_residual = dual_rhs - assemble(comply(compliance, multipliers))
    return (multipliers, final_residual)
```

```python
import jax
import jax.numpy as jnp
from jax import lax
from jax.sharding import PartitionSpec as P

HIGHEST = lax.Precision.HIGHEST
AXES = ("gx", "gy", "gz")
PLANE = ("gy", "gz")
bf16 = jnp.bfloat16


def to_all(block, axis):
    return lax.all_to_all(
        jnp.broadcast_to(block[None], (lax.axis_size(axis),) + block.shape), axis, 0, 0, tiled=True
    )


def neighbours(to_lower, to_upper):
    arrived = []
    for d, axis in enumerate(AXES):
        size = lax.axis_size(axis)
        up = [(i, i + 1) for i in range(size - 1)]
        down = [(j, i) for i, j in up]
        arrived.append(lax.ppermute(to_upper[d], axis, up))
        arrived.append(lax.ppermute(to_lower[d], axis, down))
    return arrived


def gram_solve(matrix, target):
    factor = jnp.linalg.cholesky(matrix)
    middle = lax.linalg.triangular_solve(factor, target, left_side=True, lower=True)
    return lax.linalg.triangular_solve(factor, middle, left_side=True, lower=True, transpose_a=True)


def body(compliance, rigid_modes, coarse_inverse, coarse_rhs, dual_rhs):
    face, loads = dual_rhs.shape[-1], dual_rhs.shape[-2]
    modes = rigid_modes.shape[3]
    long, plane = lax.axis_size("gx"), lax.axis_size(PLANE)
    parts = long * plane
    order = 6 * face
    matrix = compliance[0, 0, 0]
    traces = rigid_modes[0, 0, 0].reshape(modes, 6, face)
    gaps = dual_rhs[0, 0, 0].reshape(6, loads, face)
    inside = jnp.stack(
        [flag for axis in AXES for flag in (lax.axis_index(axis) > 0, jnp.bool_(True))]
    )[:, None, None]

    def gather(right_side):
        flat = right_side.astype(bf16).reshape(1, modes * loads)
        column = to_all(flat, "gx").reshape(long, modes * loads)
        return to_all(column, PLANE).reshape(parts, modes * loads)

    start = gather(coarse_rhs[0, 0, 0])

    rows = coarse_inverse.reshape(modes, long, plane, modes).transpose(0, 3, 2, 1)
    rows = rows.reshape(modes, modes * parts)
    packed = [
        jnp.concatenate([rows, traces[:, f]], axis=1) for f in range(6)
    ]
    arrived = neighbours(packed[0::2], packed[1::2])
    all_rows = jnp.concatenate([rows] + [a[:, : modes * parts] for a in arrived], axis=0)
    all_rows = all_rows.reshape(7 * modes, modes // 2, 2, parts).transpose(1, 2, 0, 3)
    all_rows = all_rows.reshape(modes // 2, 14 * modes, parts)
    high = lax.reduce_precision(all_rows, 8, 7)
    rest = all_rows - high
    middle = lax.reduce_precision(rest, 8, 7)
    pieces = jnp.concatenate([high, middle, rest - middle], axis=1).astype(bf16)
    spread = jnp.stack(
        [
            jnp.concatenate([traces[:, f], -arrived[f][:, modes * parts :]], axis=0)
            for f in range(6)
        ]
    )
    spread = jnp.where(inside, spread, 0.0)

    def coarse(stacked):
        total = 0.0
        for q in range(modes // 2):
            columns = stacked[:, 2 * loads * q : 2 * loads * (q + 1)]
            total = total + jnp.dot(pieces[q], columns, preferred_element_type=jnp.float32)
        total = total.reshape(3, 2, 7, modes, 2 * loads)
        total = total[0] + (total[1] + total[2])
        weights = total[0, :, :, :loads] + total[1, :, :, loads:]
        both = jnp.concatenate(
            [jnp.broadcast_to(weights[:1], (6, modes, loads)), weights[1:]], axis=1
        )
        return jnp.einsum("fkn,fkd->fnd", both, spread, precision=HIGHEST)

    def comply(values):
        wide = jnp.concatenate([values[f] for f in range(6)], axis=1)
        return jnp.dot(wide, matrix, precision=HIGHEST)

    def assemble(wide):
        values = [wide[:, face * f : face * (f + 1)] for f in range(6)]
        across = neighbours(values[0::2], values[1::2])
        return jnp.where(inside, jnp.stack([v - a for v, a in zip(values, across)]), 0.0)

    multipliers = coarse(start)
    residual = gaps - assemble(comply(multipliers))
    right_side = jnp.einsum("mfd,fnd->mn", traces, residual, precision=HIGHEST)
    projected = residual - coarse(gather(right_side))
    image = comply(projected)

    curvature = sum(
        jnp.dot(projected[f], image[:, face * f : face * (f + 1)].T, precision=HIGHEST)
        for f in range(6)
    )
    plus = projected[1::2]
    alignment = jnp.einsum("ind,imd->nm", plus, plus, precision=HIGHEST)
    grams = jnp.concatenate([curvature, alignment], axis=1)
    grams = lax.all_to_all(
        grams.reshape(plane, loads // plane, 2 * loads), PLANE, 0, 0, tiled=True
    ).sum(0)
    grams = to_all(grams, "gx").sum(0)
    grams = to_all(grams, PLANE).reshape(loads, 2 * loads)

    applied = assemble(image)
    step_size = gram_solve(grams[:, :loads], grams[:, loads:])
    multipliers = multipliers + jnp.einsum(
        "fnd,nm->fmd", projected, step_size, precision=HIGHEST
    )
    final_residual = residual - jnp.einsum("fnd,nm->fmd", applied, step_size, precision=HIGHEST)
    shape = (1, 1, 1, 3, 2, loads, face)
    return multipliers.reshape(shape), final_residual.reshape(shape)


def solution(mesh):
    placed = (
        P("gx", "gy", "gz", None, None),
        P("gx", "gy", "gz", None, None, None, None),
        P(AXES, None),
        P("gx", "gy", "gz", None, None),
        P("gx", "gy", "gz", None, None, None, None),
    )
    return jax.shard_map(
        body,
        mesh=mesh,
        in_specs=placed,
        out_specs=(
            P("gx", "gy", "gz", None, None, None, None),
            P("gx", "gy", "gz", None, None, None, None),
        ),
        check_vma=False,
    )
```

```python
import functools

import jax
import jax.numpy as jnp
from jax import lax
from jax.experimental import pallas as pl
from jax.sharding import PartitionSpec as P


HIGHEST = lax.Precision.HIGHEST
AXES = ("gx", "gy", "gz")
PLANE = ("gy", "gz")
bf16 = jnp.bfloat16


def to_all(block, axis):
    return lax.all_to_all(
        jnp.broadcast_to(block[None], (lax.axis_size(axis),) + block.shape), axis, 0, 0, tiled=True
    )


def neighbours(to_lower, to_upper):
    arrived = []
    for d, axis in enumerate(AXES):
        size = lax.axis_size(axis)
        up = [(i, i + 1) for i in range(size - 1)]
        down = [(j, i) for i, j in up]
        arrived.append(lax.ppermute(to_upper[d], axis, up))
        arrived.append(lax.ppermute(to_lower[d], axis, down))
    return arrived


def build_kernel(modes, parts, *refs):
    own, arrived, (pieces, spread) = refs[0], refs[1:7], refs[7:]
    every = (own,) + arrived
    width = modes * parts
    height = 14 * 8
    for q in range(modes // 2):
        for t in range(7):
            blocks = []
            for g in (2 * t, 2 * t + 1):
                half, source = divmod(g, 7)
                begin = (2 * q + half) * parts
                blocks.append(every[source][:, begin : begin + parts])
            value = jnp.concatenate(blocks, axis=0)
            for piece in range(3):
                rounded = value.astype(bf16)
                pieces[q, piece * height + 16 * t : piece * height + 16 * (t + 1), :] = rounded
                value = value - rounded.astype(jnp.float32)
    for f in range(6):
        spread[f, 0:8, :] = own[:, width + 128 * f : width + 128 * (f + 1)]
        spread[f, 8:16, :] = -arrived[f][:, width : width + 128]


def solve_kernel(grams, solution):
    size = grams.shape[0]
    table = grams[...]
    row_index = lax.broadcasted_iota(jnp.int32, table.shape, 0)
    for k in range(size):
        pivot = table[k : k + 1, :] / table[k : k + 1, k : k + 1]
        column = table[:, k : k + 1]
        table = jnp.where(row_index == k, pivot, table - column * pivot)
    solution[...] = table[:, size:]


def gram_solve(grams):
    size = grams.shape[0]
    return pl.pallas_call(
        solve_kernel, out_shape=jax.ShapeDtypeStruct((size, size), jnp.float32), name="gram_solve"
    )(grams)


def body(compliance, rigid_modes, coarse_inverse, coarse_rhs, dual_rhs):
    face, loads = dual_rhs.shape[-1], dual_rhs.shape[-2]
    modes = rigid_modes.shape[3]
    long, plane = lax.axis_size("gx"), lax.axis_size(PLANE)
    parts = long * plane
    order = 6 * face
    matrix = compliance[0, 0, 0]
    traces = rigid_modes[0, 0, 0].reshape(modes, 6, face)
    gaps = dual_rhs[0, 0, 0].reshape(6, loads, face)
    inside = jnp.stack(
        [flag for axis in AXES for flag in (lax.axis_index(axis) > 0, jnp.bool_(True))]
    )[:, None, None]

    def gather(right_side):
        flat = right_side.astype(bf16).reshape(1, modes * loads)
        column = to_all(flat, "gx").reshape(long, modes * loads)
        return to_all(column, PLANE).reshape(parts, modes * loads)

    flat = coarse_rhs[0, 0, 0].astype(bf16).reshape(1, modes * loads)
    column = to_all(flat, "gx").reshape(long, modes * loads)
    start = to_all(column, PLANE).reshape(parts, modes * loads)

    rows = coarse_inverse.reshape(modes, long, plane, modes).transpose(0, 3, 2, 1)
    rows = jnp.pad(rows.reshape(modes, modes * parts), ((0, 8 - modes), (0, 0)))
    padded = jnp.pad(traces, ((0, 8 - modes), (0, 0), (0, 0)))
    packed = [jnp.concatenate([rows, padded[:, f]], axis=1) for f in range(6)]
    own = jnp.concatenate([rows, padded.reshape(8, order)], axis=1)
    arrived = neighbours(packed[0::2], packed[1::2])
    pieces, spread = pl.pallas_call(
        functools.partial(build_kernel, modes, parts),
        out_shape=(
            jax.ShapeDtypeStruct((modes // 2, 3 * 14 * 8, parts), bf16),
            jax.ShapeDtypeStruct((6, 16, face), jnp.float32),
        ),
        name="build_rows",
    )(own, *arrived)
    spread = jnp.where(inside, spread, 0.0)

    def coarse(stacked):
        total = 0.0
        for q in range(modes // 2):
            columns = stacked[:, 2 * loads * q : 2 * loads * (q + 1)]
            total = total + jnp.dot(pieces[q], columns, preferred_element_type=jnp.float32)
        total = total.reshape(3, 2, 7, 8, 2 * loads)
        total = total[0] + (total[1] + total[2])
        weights = total[0, :, :, :loads] + total[1, :, :, loads:]
        both = jnp.concatenate(
            [jnp.broadcast_to(weights[:1], (6, 8, loads)), weights[1:]], axis=1
        )
        return jnp.einsum("fkn,fkd->fnd", both, spread, precision=HIGHEST)

    def comply(values):
        wide = jnp.concatenate([values[f] for f in range(6)], axis=1)
        return jnp.dot(wide, matrix, precision=HIGHEST)

    def assemble(wide):
        values = [wide[:, face * f : face * (f + 1)] for f in range(6)]
        across = neighbours(values[0::2], values[1::2])
        return jnp.where(inside, jnp.stack([v - a for v, a in zip(values, across)]), 0.0)

    multipliers = coarse(start)
    residual = gaps - assemble(comply(multipliers))
    right_side = jnp.einsum("mfd,fnd->mn", traces, residual, precision=HIGHEST)
    projected = residual - coarse(gather(right_side))
    image = comply(projected)

    curvature = sum(
        jnp.dot(projected[f], image[:, face * f : face * (f + 1)].T, precision=HIGHEST)
        for f in range(6)
    )
    plus = projected[1::2]
    alignment = jnp.einsum("ind,imd->nm", plus, plus, precision=HIGHEST)
    grams = jnp.concatenate([curvature, alignment], axis=1)
    grams = lax.all_to_all(
        grams.reshape(plane, loads // plane, 2 * loads), PLANE, 0, 0, tiled=True
    ).sum(0)
    grams = to_all(grams, "gx").sum(0)
    grams = to_all(grams, PLANE).reshape(loads, 2 * loads)

    applied = assemble(image)
    step_size = gram_solve(grams)
    multipliers = multipliers + jnp.einsum(
        "fnd,nm->fmd", projected, step_size, precision=HIGHEST
    )
    final_residual = residual - jnp.einsum("fnd,nm->fmd", applied, step_size, precision=HIGHEST)
    shape = (1, 1, 1, 3, 2, loads, face)
    return multipliers.reshape(shape), final_residual.reshape(shape)


def solution(mesh):
    placed = (
        P("gx", "gy", "gz", None, None),
        P("gx", "gy", "gz", None, None, None, None),
        P(AXES, None),
        P("gx", "gy", "gz", None, None),
        P("gx", "gy", "gz", None, None, None, None),
    )

    return jax.shard_map(
        body,
        mesh=mesh,
        in_specs=placed,
        out_specs=(
            P("gx", "gy", "gz", None, None, None, None),
            P("gx", "gy", "gz", None, None, None, None),
        ),
        check_vma=False,
    )
```

```python
import functools

import jax
import jax.numpy as jnp
from jax import lax
from jax.experimental import pallas as pl
from jax.experimental.pallas import tpu as pltpu
from jax.sharding import PartitionSpec as P


HIGHEST = lax.Precision.HIGHEST
AXES = ("gx", "gy", "gz")
PLANE = ("gy", "gz")
bf16 = jnp.bfloat16
f32 = jnp.float32


def to_all(block, axis):
    return lax.all_to_all(
        jnp.broadcast_to(block[None], (lax.axis_size(axis),) + block.shape), axis, 0, 0, tiled=True
    )


def swap(outgoing):
    arrived = []
    for d, axis in enumerate(AXES):
        size = lax.axis_size(axis)
        even = [(i, i ^ 1) for i in range(size)]
        odd = [(i, i + 1 if i % 2 else i - 1) for i in range(1, size - 1)]
        arrived.append(lax.ppermute(outgoing[2 * d], axis, even))
        arrived.append(lax.ppermute(outgoing[2 * d + 1], axis, odd))
    return arrived


def pick(is_even, f, pair):
    even, odd = pair
    first, second = (odd, even) if f % 2 == 0 else (even, odd)
    return jnp.where(is_even, first, second)


def prepare(modes, long, plane, flags, rows, traces, *packed):
    turned = packed[-1]
    packed = packed[:-1]
    parts = long * plane
    blank = jnp.zeros((8 - modes, 128), f32)
    for b in range(modes * parts // 128):
        block = jnp.concatenate([rows[:, 128 * b : 128 * (b + 1)], blank], axis=0)
        turned[128 * b : 128 * (b + 1), :] = block.T
    group = 128 // long
    for j in range(modes):
        for b in range(parts // 128):
            strips = [
                turned[pl.ds((group * b + i) * modes + j, long, stride=plane * modes), :]
                for i in range(group)
            ]
            block = jnp.concatenate(strips, axis=0).T
            begin = j * parts + 128 * b
            for out in packed:
                out[:, begin : begin + 128] = block
    for d in range(3):
        is_even = flags[d] == 0
        minus = jnp.concatenate([traces[2 * d], blank], axis=0)
        plus = jnp.concatenate([traces[2 * d + 1], blank], axis=0)
        packed[2 * d][:, modes * parts :] = jnp.where(is_even, plus, minus)
        packed[2 * d + 1][:, modes * parts :] = jnp.where(is_even, minus, plus)


def build(modes, parts, flags, traces, own, *refs):
    arrived, (pieces, spread) = refs[:6], refs[6:]
    width = modes * parts
    height = 14 * 8
    evens = [flags[d] == 0 for d in range(3)]
    blank = jnp.zeros((8 - modes, 128), f32)

    def take(source, begin, size):
        if source == 0:
            return own[:, begin : begin + size]
        f = source - 1
        pair = [r[:, begin : begin + size] for r in arrived[2 * (f // 2) : 2 * (f // 2) + 2]]
        return pick(evens[f // 2], f, pair)

    for q in range(modes // 2):
        for t in range(7):
            blocks = []
            for g in (2 * t, 2 * t + 1):
                half, source = divmod(g, 7)
                blocks.append(take(source, (2 * q + half) * parts, parts))
            value = jnp.concatenate(blocks, axis=0)
            for piece in range(3):
                rounded = value.astype(bf16)
                pieces[q, piece * height + 16 * t : piece * height + 16 * (t + 1), :] = rounded
                value = value - rounded.astype(f32)
    spread[...] = jnp.zeros_like(spread)
    for f in range(6):
        lanes = slice(128 * f, 128 * (f + 1))
        mine = jnp.concatenate([traces[f], blank], axis=0)
        other = -take(f + 1, width, 128)
        if f % 2 == 0:
            inside = flags[3 + f // 2] > 0
            mine = jnp.where(inside, mine, 0.0)
            other = jnp.where(inside, other, 0.0)
        spread[0:8, lanes] = mine
        spread[8 * (f + 1) : 8 * (f + 2), lanes] = other


def coarse(stacked, pieces, spread):
    lanes = stacked.shape[1] // pieces.shape[0]
    total = jnp.zeros((pieces.shape[1], lanes), f32)
    for q in range(pieces.shape[0]):
        total = total + jnp.dot(
            pieces[q], stacked[:, lanes * q : lanes * (q + 1)], preferred_element_type=f32
        )
    height = pieces.shape[1] // 3
    total = total[:height] + (total[height : 2 * height] + total[2 * height :])
    weights = total[: height // 2, : lanes // 2] + total[height // 2 :, lanes // 2 :]
    return jnp.dot(weights.T, spread[...], precision=HIGHEST, preferred_element_type=f32)


def send_faces(flags, wide, outgoing):
    for d in range(3):
        minus = wide[:, 256 * d : 256 * d + 128]
        plus = wide[:, 256 * d + 128 : 256 * d + 256]
        outgoing[2 * d][...] = jnp.where(flags[d] == 0, plus, minus)
        outgoing[2 * d + 1][...] = jnp.where(flags[d] == 0, minus, plus)


def assembled(flags, wide, arrived, f):
    d = f // 2
    pair = (arrived[2 * d][...], arrived[2 * d + 1][...])
    value = wide[:, 128 * f : 128 * (f + 1)] - pick(flags[d] == 0, f, pair)
    return jnp.where(flags[3 + d] > 0, value, 0.0) if f % 2 == 0 else value


def start_kernel(flags, stacked, pieces, spread, matrix, field, image, *outgoing):
    value = coarse(stacked, pieces, spread)
    field[...] = value
    image[...] = jnp.dot(value, matrix[...], precision=HIGHEST, preferred_element_type=f32)
    send_faces(flags, image, outgoing)


def residual_kernel(flags, gaps, traces, image, *refs):
    arrived, (residual, sums) = refs[:6], refs[6:]
    total = 0.0
    for f in range(6):
        value = gaps[f] - assembled(flags, image, arrived, f)
        residual[:, 128 * f : 128 * (f + 1)] = value
        total = total + lax.dot_general(
            traces[f], value, (((1,), (1,)), ((), ())), precision=HIGHEST, preferred_element_type=f32
        )
    sums[...] = total.astype(bf16)


def project_kernel(flags, stacked, pieces, spread, matrix, residual, field, image, grams, *outgoing):
    value = residual[...] - coarse(stacked, pieces, spread)
    field[...] = value
    applied = jnp.dot(value, matrix[...], precision=HIGHEST, preferred_element_type=f32)
    image[...] = applied
    across = (((1,), (1,)), ((), ()))
    loads = value.shape[0]
    grams[:, :loads] = lax.dot_general(
        value, applied, across, precision=HIGHEST, preferred_element_type=f32
    )
    plus = jnp.concatenate([value[:, 256 * d + 128 : 256 * d + 256] for d in range(3)], axis=1)
    grams[:, loads:] = lax.dot_general(
        plus, plus, across, precision=HIGHEST, preferred_element_type=f32
    )
    send_faces(flags, image, outgoing)


def solve(table):
    size = table.shape[0]
    row = lax.broadcasted_iota(jnp.int32, table.shape, 0)
    for k in range(0, size, 2):
        first, second = table[k : k + 1, :], table[k + 1 : k + 2, :]
        left, right = table[:, k : k + 1], table[:, k + 1 : k + 2]
        inverse = 1.0 / left[k : k + 1]
        ratio = left[k + 1 : k + 2] * inverse
        corner = 1.0 / (right[k + 1 : k + 2] - ratio * right[k : k + 1])
        lower = (second - ratio * first) * corner
        upper = (first - right[k : k + 1] * lower) * inverse
        table = jnp.where(
            row == k, upper, jnp.where(row == k + 1, lower, table - left * upper - right * lower)
        )
    return table[:, size:]


def final_kernel(flags, grams, multipliers, residual, field, image, *refs):
    arrived, (new_multipliers, new_residual) = refs[:6], refs[6:]
    step = solve(grams[...]).T
    change = jnp.dot(step, field[...], precision=HIGHEST, preferred_element_type=f32)
    for f in range(6):
        lanes = slice(128 * f, 128 * (f + 1))
        new_multipliers[f] = multipliers[:, lanes] + change[:, lanes]
        applied = assembled(flags, image, arrived, f)
        new_residual[f] = residual[:, lanes] - jnp.dot(
            step, applied, precision=HIGHEST, preferred_element_type=f32
        )


def call(kernel, outs, *args, **options):
    flags = pl.BlockSpec(memory_space=pltpu.SMEM)
    block = pl.BlockSpec(memory_space=pltpu.VMEM)
    return pl.pallas_call(
        kernel,
        out_shape=[jax.ShapeDtypeStruct(shape, kind) for shape, kind in outs],
        in_specs=[flags] + [block] * (len(args) - 1),
        out_specs=[block] * len(outs),
        compiler_params=pltpu.CompilerParams(vmem_limit_bytes=24 << 20),
        **options,
    )(*args)


def body(compliance, rigid_modes, coarse_inverse, coarse_rhs, dual_rhs):
    face, loads = dual_rhs.shape[-1], dual_rhs.shape[-2]
    modes = rigid_modes.shape[3]
    long, plane = lax.axis_size("gx"), lax.axis_size(PLANE)
    parts = long * plane
    matrix = compliance[0, 0, 0]
    traces = rigid_modes[0, 0, 0].transpose(1, 2, 0, 3).reshape(6, modes, face)
    gaps = dual_rhs[0, 0, 0].reshape(6, loads, face)
    where = [lax.axis_index(axis) for axis in AXES]
    flags = jnp.stack([w % 2 for w in where] + [jnp.minimum(w, 1) for w in where]).astype(jnp.int32)
    wide, faces = ((loads, 6 * face), f32), ((6, loads, face), f32)
    packs = ((8, modes * parts + face), f32)

    def along(sums):
        return to_all(sums.astype(bf16).reshape(1, modes * loads), "gx").reshape(long, modes * loads)

    def across(column):
        return to_all(column, PLANE).reshape(parts, modes * loads)

    column = along(coarse_rhs[0, 0, 0])
    packed = call(
        functools.partial(prepare, modes, long, plane),
        [packs] * 6,
        flags,
        coarse_inverse,
        traces,
        scratch_shapes=[pltpu.VMEM((modes * parts, 8), f32)],
        name="prepare_rows",
    )
    arrived = swap(packed)
    stacked = across(column)
    pieces, spread = call(
        functools.partial(build, modes, parts),
        [((modes // 2, 3 * 14 * 8, parts), bf16), ((7 * 8, 6 * face), f32)],
        flags,
        traces,
        packed[0],
        *arrived,
        name="build_rows",
    )

    multipliers, image, *outgoing = call(
        start_kernel,
        [wide, wide] + [((loads, face), f32)] * 6,
        flags,
        stacked,
        pieces,
        spread,
        matrix,
        name="start_fields",
    )
    residual, sums = call(
        residual_kernel,
        [wide, ((modes, loads), bf16)],
        flags,
        gaps,
        traces,
        image,
        *swap(outgoing),
        name="residual",
    )
    projected, image, grams, *outgoing = call(
        project_kernel,
        [wide, wide, ((loads, 2 * loads), f32)] + [((loads, face), f32)] * 6,
        flags,
        across(along(sums)),
        pieces,
        spread,
        matrix,
        residual,
        name="project",
    )
    grams = lax.all_to_all(
        grams.reshape(plane, loads // plane, 2 * loads), PLANE, 0, 0, tiled=True
    ).sum(0)
    grams = to_all(grams, "gx").sum(0)
    grams = to_all(grams, PLANE).reshape(loads, 2 * loads)
    arrived = swap(outgoing)
    outputs = call(
        final_kernel,
        [faces, faces],
        flags,
        grams,
        multipliers,
        residual,
        projected,
        image,
        *arrived,
        name="final_update",
    )
    return tuple(out.reshape(1, 1, 1, 3, 2, loads, face) for out in outputs)


def solution(mesh):
    placed = (
        P("gx", "gy", "gz", None, None),
        P("gx", "gy", "gz", None, None, None, None),
        P(AXES, None),
        P("gx", "gy", "gz", None, None),
        P("gx", "gy", "gz", None, None, None, None),
    )

    return jax.shard_map(
        body,
        mesh=mesh,
        in_specs=placed,
        out_specs=(
            P("gx", "gy", "gz", None, None, None, None),
            P("gx", "gy", "gz", None, None, None, None),
        ),
        check_vma=False,
    )
```

```python
import functools

import jax
import jax.numpy as jnp
from jax import lax
from jax.experimental import pallas as pl
from jax.experimental.pallas import tpu as pltpu
from jax.sharding import PartitionSpec as P


HIGHEST = lax.Precision.HIGHEST
AXES = ("gx", "gy", "gz")
PLANE = ("gy", "gz")
bf16 = jnp.bfloat16
f32 = jnp.float32


def to_all(block, axis):
    return lax.all_to_all(
        jnp.broadcast_to(block[None], (lax.axis_size(axis),) + block.shape), axis, 0, 0, tiled=True
    )


def swap(outgoing, axes=AXES):
    arrived = []
    for d, axis in enumerate(axes):
        size = lax.axis_size(axis)
        even = [(i, i ^ 1) for i in range(size)]
        odd = [(i, i + 1 if i % 2 else i - 1) for i in range(1, size - 1)]
        arrived.append(lax.ppermute(outgoing[2 * d], axis, even))
        arrived.append(lax.ppermute(outgoing[2 * d + 1], axis, odd))
    return arrived


def pick(is_even, f, pair):
    even, odd = pair
    first, second = (odd, even) if f % 2 == 0 else (even, odd)
    return jnp.where(is_even, first, second)


def prepare(modes, long, plane, flags, rows, traces, *packed):
    turned = packed[-1]
    packed = packed[:-1]
    parts = long * plane
    blank = jnp.zeros((8 - modes, 128), f32)
    for b in range(modes * parts // 128):
        block = jnp.concatenate([rows[:, 128 * b : 128 * (b + 1)], blank], axis=0)
        turned[128 * b : 128 * (b + 1), :] = block.T
    group = 128 // long
    for j in range(modes):
        for b in range(parts // 128):
            strips = [
                turned[pl.ds((group * b + i) * modes + j, long, stride=plane * modes), :]
                for i in range(group)
            ]
            block = jnp.concatenate(strips, axis=0).T
            begin = j * parts + 128 * b
            for out in packed:
                out[:, begin : begin + 128] = block
    for d in range(3):
        is_even = flags[d] == 0
        minus = jnp.concatenate([traces[2 * d], blank], axis=0)
        plus = jnp.concatenate([traces[2 * d + 1], blank], axis=0)
        packed[2 * d][:, modes * parts :] = jnp.where(is_even, plus, minus)
        packed[2 * d + 1][:, modes * parts :] = jnp.where(is_even, minus, plus)


def build(modes, parts, flags, traces, own, *refs):
    arrived, (pieces, spread) = refs[:6], refs[6:]
    width = modes * parts
    height = 14 * 8
    evens = [flags[d] == 0 for d in range(3)]
    blank = jnp.zeros((8 - modes, 128), f32)

    def take(source, begin, size):
        if source == 0:
            return own[:, begin : begin + size]
        f = source - 1
        pair = [r[:, begin : begin + size] for r in arrived[2 * (f // 2) : 2 * (f // 2) + 2]]
        return pick(evens[f // 2], f, pair)

    for q in range(modes // 2):
        for t in range(7):
            blocks = []
            for g in (2 * t, 2 * t + 1):
                half, source = divmod(g, 7)
                blocks.append(take(source, (2 * q + half) * parts, parts))
            value = jnp.concatenate(blocks, axis=0)
            for piece in range(3):
                rounded = value.astype(bf16)
                pieces[q, piece * height + 16 * t : piece * height + 16 * (t + 1), :] = rounded
                value = value - rounded.astype(f32)
    spread[...] = jnp.zeros_like(spread)
    for f in range(6):
        lanes = slice(128 * f, 128 * (f + 1))
        mine = jnp.concatenate([traces[f], blank], axis=0)
        other = -take(f + 1, width, 128)
        if f % 2 == 0:
            inside = flags[3 + f // 2] > 0
            mine = jnp.where(inside, mine, 0.0)
            other = jnp.where(inside, other, 0.0)
        spread[0:8, lanes] = mine
        spread[8 * (f + 1) : 8 * (f + 2), lanes] = other


def coarse(stacked, pieces, spread):
    lanes = stacked.shape[1] // pieces.shape[0]
    total = jnp.zeros((pieces.shape[1], lanes), f32)
    for q in range(pieces.shape[0]):
        total = total + jnp.dot(
            pieces[q], stacked[:, lanes * q : lanes * (q + 1)], preferred_element_type=f32
        )
    height = pieces.shape[1] // 3
    total = total[:height] + (total[height : 2 * height] + total[2 * height :])
    weights = total[: height // 2, : lanes // 2] + total[height // 2 :, lanes // 2 :]
    return jnp.dot(weights.T, spread[...], precision=HIGHEST, preferred_element_type=f32)


def send_faces(flags, wide, outgoing):
    for d in range(3):
        minus = wide[:, 256 * d : 256 * d + 128]
        plus = wide[:, 256 * d + 128 : 256 * d + 256]
        outgoing[2 * d][...] = jnp.where(flags[d] == 0, plus, minus)
        outgoing[2 * d + 1][...] = jnp.where(flags[d] == 0, minus, plus)


def assembled(flags, wide, arrived, f):
    d = f // 2
    pair = (arrived[2 * d][...], arrived[2 * d + 1][...])
    value = wide[:, 128 * f : 128 * (f + 1)] - pick(flags[d] == 0, f, pair)
    return jnp.where(flags[3 + d] > 0, value, 0.0) if f % 2 == 0 else value


def as_rows(sums, out):
    modes, loads = sums.shape
    rows = [jnp.concatenate([sums[m : m + 1], sums[m + 1 : m + 2]], axis=1) for m in range(0, modes, 2)]
    rows = jnp.concatenate(rows + [jnp.zeros((1, 2 * loads), f32)], axis=0)
    out[...] = jnp.broadcast_to(rows[None], out.shape).astype(bf16)


def modes_kernel(flags, right_side, out):
    as_rows(right_side[...], out)


def widen_kernel(flags, column, out):
    value = column[...].astype(f32)
    wide = jnp.concatenate([value[:, q, :] for q in range(value.shape[1] - 1)], axis=1).astype(bf16)
    for p in range(out.shape[0]):
        out[p] = wide


def start_kernel(flags, stacked, pieces, spread, matrix, field, image, *outgoing):
    value = coarse(stacked, pieces, spread)
    field[...] = value
    image[...] = jnp.dot(value, matrix[...], precision=HIGHEST, preferred_element_type=f32)
    send_faces(flags, image, outgoing)


def residual_kernel(flags, gaps, traces, image, *refs):
    arrived, (residual, sums) = refs[:6], refs[6:]
    total = 0.0
    for f in range(6):
        value = gaps[f] - assembled(flags, image, arrived, f)
        residual[:, 128 * f : 128 * (f + 1)] = value
        total = total + lax.dot_general(
            traces[f], value, (((1,), (1,)), ((), ())), precision=HIGHEST, preferred_element_type=f32
        )
    as_rows(total, sums)


def project_kernel(flags, stacked, pieces, spread, matrix, residual, field, image, grams, *outgoing):
    value = residual[...] - coarse(stacked, pieces, spread)
    field[...] = value
    applied = jnp.dot(value, matrix[...], precision=HIGHEST, preferred_element_type=f32)
    image[...] = applied
    across = (((1,), (1,)), ((), ()))
    loads = value.shape[0]
    grams[:, :loads] = lax.dot_general(
        value, applied, across, precision=HIGHEST, preferred_element_type=f32
    )
    plus = jnp.concatenate([value[:, 256 * d + 128 : 256 * d + 256] for d in range(3)], axis=1)
    grams[:, loads:] = lax.dot_general(
        plus, plus, across, precision=HIGHEST, preferred_element_type=f32
    )
    send_faces(flags, image, outgoing)


def solve(table):
    size = table.shape[0]
    row = lax.broadcasted_iota(jnp.int32, table.shape, 0)
    for begin in range(0, size, 4):
        columns = [
            jnp.broadcast_to(table[:, k : k + 1], table.shape) for k in range(begin, begin + 4)
        ]
        for i in range(4):
            k = begin + i
            column = columns[i]
            inverse = 1.0 / column[k : k + 1]
            pivot = table[k : k + 1] * inverse
            table = jnp.where(row == k, pivot, table - column * pivot)
            for j in range(i + 1, 4):
                pivot = columns[j][k : k + 1] * inverse
                columns[j] = jnp.where(row == k, pivot, columns[j] - column * pivot)
    return table[:, size:]


def final_kernel(flags, grams, multipliers, residual, field, image, *refs):
    arrived, (new_multipliers, new_residual) = refs[:6], refs[6:]
    step = solve(grams[...]).T
    change = jnp.dot(step, field[...], precision=HIGHEST, preferred_element_type=f32)
    for f in range(6):
        lanes = slice(128 * f, 128 * (f + 1))
        new_multipliers[f] = multipliers[:, lanes] + change[:, lanes]
        applied = assembled(flags, image, arrived, f)
        new_residual[f] = residual[:, lanes] - jnp.dot(
            step, applied, precision=HIGHEST, preferred_element_type=f32
        )


def call(kernel, outs, *args, **options):
    flags = pl.BlockSpec(memory_space=pltpu.SMEM)
    block = pl.BlockSpec(memory_space=pltpu.VMEM)
    return pl.pallas_call(
        kernel,
        out_shape=[jax.ShapeDtypeStruct(shape, kind) for shape, kind in outs],
        in_specs=[flags] + [block] * (len(args) - 1),
        out_specs=[block] * len(outs),
        compiler_params=pltpu.CompilerParams(vmem_limit_bytes=24 << 20),
        **options,
    )(*args)


def body(compliance, rigid_modes, coarse_inverse, coarse_rhs, dual_rhs):
    face, loads = dual_rhs.shape[-1], dual_rhs.shape[-2]
    modes = rigid_modes.shape[3]
    long, plane = lax.axis_size("gx"), lax.axis_size(PLANE)
    parts = long * plane
    matrix = compliance[0, 0, 0]
    traces = rigid_modes[0, 0, 0].transpose(1, 2, 0, 3).reshape(6, modes, face)
    gaps = dual_rhs[0, 0, 0].reshape(6, loads, face)
    where = [lax.axis_index(axis) for axis in AXES]
    flags = jnp.stack([w % 2 for w in where] + [jnp.minimum(w, 1) for w in where]).astype(jnp.int32)
    wide, faces = ((loads, 6 * face), f32), ((6, loads, face), f32)
    packs = ((8, modes * parts + face), f32)

    row = ((long, modes // 2 + 1, 2 * loads), bf16)

    def along(rows):
        return lax.all_to_all(rows, "gx", 0, 0, tiled=True)

    def across(column):
        column = call(
            widen_kernel, [((plane, long, modes * loads), bf16)], flags, column, name="widen"
        )[0]
        return lax.all_to_all(column, PLANE, 0, 0, tiled=True).reshape(parts, modes * loads)

    column = along(call(modes_kernel, [row], flags, coarse_rhs[0, 0, 0], name="modes")[0])
    packed = call(
        functools.partial(prepare, modes, long, plane),
        [packs] * 6,
        flags,
        coarse_inverse,
        traces,
        scratch_shapes=[pltpu.VMEM((modes * parts, 8), f32)],
        name="prepare_rows",
    )
    in_plane = swap(packed[2:], PLANE)
    arrived = swap(packed[:2], AXES[:1]) + in_plane
    stacked = across(column)
    pieces, spread = call(
        functools.partial(build, modes, parts),
        [((modes // 2, 3 * 14 * 8, parts), bf16), ((7 * 8, 6 * face), f32)],
        flags,
        traces,
        packed[0],
        *arrived,
        name="build_rows",
    )

    multipliers, image, *outgoing = call(
        start_kernel,
        [wide, wide] + [((loads, face), f32)] * 6,
        flags,
        stacked,
        pieces,
        spread,
        matrix,
        name="start_fields",
    )
    residual, sums = call(
        residual_kernel,
        [wide, row],
        flags,
        gaps,
        traces,
        image,
        *swap(outgoing),
        name="residual",
    )
    projected, image, grams, *outgoing = call(
        project_kernel,
        [wide, wide, ((loads, 2 * loads), f32)] + [((loads, face), f32)] * 6,
        flags,
        across(along(sums)),
        pieces,
        spread,
        matrix,
        residual,
        name="project",
    )
    grams = lax.all_to_all(
        grams.reshape(plane, loads // plane, 2 * loads), PLANE, 0, 0, tiled=True
    ).sum(0)
    grams = to_all(grams, "gx").sum(0)
    grams = to_all(grams, PLANE).reshape(loads, 2 * loads)
    arrived = swap(outgoing)
    outputs = call(
        final_kernel,
        [faces, faces],
        flags,
        grams,
        multipliers,
        residual,
        projected,
        image,
        *arrived,
        name="final_update",
    )
    return tuple(out.reshape(1, 1, 1, 3, 2, loads, face) for out in outputs)


def solution(mesh):
    placed = (
        P("gx", "gy", "gz", None, None),
        P("gx", "gy", "gz", None, None, None, None),
        P(AXES, None),
        P("gx", "gy", "gz", None, None),
        P("gx", "gy", "gz", None, None, None, None),
    )

    return jax.shard_map(
        body,
        mesh=mesh,
        in_specs=placed,
        out_specs=(
            P("gx", "gy", "gz", None, None, None, None),
            P("gx", "gy", "gz", None, None, None, None),
        ),
        check_vma=False,
    )
```

```python
import functools

import jax
import jax.numpy as jnp
from jax import lax
from jax.experimental import pallas as pl
from jax.experimental.pallas import tpu as pltpu
from jax.sharding import PartitionSpec as P


HIGHEST = lax.Precision.HIGHEST
AXES = ("gx", "gy", "gz")
PLANE = ("gy", "gz")
bf16 = jnp.bfloat16
f32 = jnp.float32


def to_all(block, axis):
    return lax.all_to_all(
        jnp.broadcast_to(block[None], (lax.axis_size(axis),) + block.shape), axis, 0, 0, tiled=True
    )


def swap(outgoing, axes=AXES):
    arrived = []
    for d, axis in enumerate(axes):
        size = lax.axis_size(axis)
        even = [(i, i ^ 1) for i in range(size)]
        odd = [(i, i + 1 if i % 2 else i - 1) for i in range(1, size - 1)]
        arrived.append(lax.ppermute(outgoing[2 * d], axis, even))
        arrived.append(lax.ppermute(outgoing[2 * d + 1], axis, odd))
    return arrived


def pick(is_even, f, pair):
    even, odd = pair
    first, second = (odd, even) if f % 2 == 0 else (even, odd)
    return jnp.where(is_even, first, second)


def prepare(modes, long, plane, flags, rows, traces, *packed):
    turned = packed[-1]
    packed = packed[:-1]
    parts = long * plane
    blank = jnp.zeros((8 - modes, 128), f32)
    for b in range(modes * parts // 128):
        block = jnp.concatenate([rows[:, 128 * b : 128 * (b + 1)], blank], axis=0)
        turned[128 * b : 128 * (b + 1), :] = block.T
    group = 128 // long
    for j in range(modes):
        for b in range(parts // 128):
            strips = [
                turned[pl.ds((group * b + i) * modes + j, long, stride=plane * modes), :]
                for i in range(group)
            ]
            block = jnp.concatenate(strips, axis=0).T
            begin = j * parts + 128 * b
            for out in packed:
                out[:, begin : begin + 128] = block
    for d in range(3):
        is_even = flags[d] == 0
        minus = jnp.concatenate([traces[:, d, 0, :], blank], axis=0)
        plus = jnp.concatenate([traces[:, d, 1, :], blank], axis=0)
        packed[2 * d][:, modes * parts :] = jnp.where(is_even, plus, minus)
        packed[2 * d + 1][:, modes * parts :] = jnp.where(is_even, minus, plus)


def build(modes, parts, flags, traces, own, *refs):
    arrived, (pieces, spread) = refs[:6], refs[6:]
    width = modes * parts
    height = 14 * 8
    evens = [flags[d] == 0 for d in range(3)]
    blank = jnp.zeros((8 - modes, 128), f32)

    def take(source, begin, size):
        if source == 0:
            return own[:, begin : begin + size]
        f = source - 1
        pair = [r[:, begin : begin + size] for r in arrived[2 * (f // 2) : 2 * (f // 2) + 2]]
        return pick(evens[f // 2], f, pair)

    for q in range(modes // 2):
        for t in range(7):
            blocks = []
            for g in (2 * t, 2 * t + 1):
                half, source = divmod(g, 7)
                blocks.append(take(source, (2 * q + half) * parts, parts))
            value = jnp.concatenate(blocks, axis=0)
            for piece in range(3):
                rounded = value.astype(bf16)
                pieces[q, piece * height + 16 * t : piece * height + 16 * (t + 1), :] = rounded
                value = value - rounded.astype(f32)
    spread[...] = jnp.zeros_like(spread)
    for f in range(6):
        lanes = slice(128 * f, 128 * (f + 1))
        mine = jnp.concatenate([traces[f], blank], axis=0)
        other = -take(f + 1, width, 128)
        if f % 2 == 0:
            inside = flags[3 + f // 2] > 0
            mine = jnp.where(inside, mine, 0.0)
            other = jnp.where(inside, other, 0.0)
        spread[0:8, lanes] = mine
        spread[8 * (f + 1) : 8 * (f + 2), lanes] = other


def coarse(stacked, pieces, spread):
    lanes = stacked.shape[1] // pieces.shape[0]
    total = jnp.zeros((pieces.shape[1], lanes), f32)
    for q in range(pieces.shape[0]):
        total = total + jnp.dot(
            pieces[q], stacked[:, lanes * q : lanes * (q + 1)], preferred_element_type=f32
        )
    height = pieces.shape[1] // 3
    total = total[:height] + (total[height : 2 * height] + total[2 * height :])
    weights = total[: height // 2, : lanes // 2] + total[height // 2 :, lanes // 2 :]
    return jnp.dot(weights.T, spread[...], precision=HIGHEST, preferred_element_type=f32)


def send_faces(flags, wide, outgoing):
    for d in range(3):
        minus = wide[:, 256 * d : 256 * d + 128]
        plus = wide[:, 256 * d + 128 : 256 * d + 256]
        outgoing[2 * d][...] = jnp.where(flags[d] == 0, plus, minus)
        outgoing[2 * d + 1][...] = jnp.where(flags[d] == 0, minus, plus)


def assembled(flags, wide, arrived, f):
    d = f // 2
    pair = (arrived[2 * d][...], arrived[2 * d + 1][...])
    value = wide[:, 128 * f : 128 * (f + 1)] - pick(flags[d] == 0, f, pair)
    return jnp.where(flags[3 + d] > 0, value, 0.0) if f % 2 == 0 else value


def as_rows(sums, out):
    modes, loads = sums.shape
    rows = [jnp.concatenate([sums[m : m + 1], sums[m + 1 : m + 2]], axis=1) for m in range(0, modes, 2)]
    rows = jnp.concatenate(rows + [jnp.zeros((1, 2 * loads), f32)], axis=0)
    out[...] = jnp.broadcast_to(rows[None], out.shape).astype(bf16)


def modes_kernel(flags, right_side, out):
    as_rows(jnp.concatenate([right_side[m] for m in range(right_side.shape[0])], axis=0), out)


def widen_kernel(flags, column, out):
    value = column[...].astype(f32)
    wide = jnp.concatenate([value[:, q, :] for q in range(value.shape[1] - 1)], axis=1).astype(bf16)
    for p in range(out.shape[0]):
        out[p] = wide


def start_kernel(flags, stacked, pieces, spread, stored, field, image, *refs):
    outgoing, (matrix, arrival) = refs[:6], refs[6:]
    copy = pltpu.make_async_copy(stored, matrix, arrival)
    copy.start()
    value = coarse(stacked, pieces, spread)
    field[...] = value
    copy.wait()
    image[...] = jnp.dot(value, matrix[...], precision=HIGHEST, preferred_element_type=f32)
    send_faces(flags, image, outgoing)


def residual_kernel(flags, gaps, traces, image, *refs):
    arrived, (residual, sums) = refs[:6], refs[6:]
    total = 0.0
    for f in range(6):
        value = gaps[f] - assembled(flags, image, arrived, f)
        residual[:, 128 * f : 128 * (f + 1)] = value
        total = total + lax.dot_general(
            traces[f], value, (((1,), (1,)), ((), ())), precision=HIGHEST, preferred_element_type=f32
        )
    as_rows(total, sums)


def project_kernel(flags, stacked, pieces, spread, stored, residual, field, image, grams, *refs):
    outgoing, (matrix, arrival) = refs[:6], refs[6:]
    copy = pltpu.make_async_copy(stored, matrix, arrival)
    copy.start()
    value = residual[...] - coarse(stacked, pieces, spread)
    field[...] = value
    copy.wait()
    applied = jnp.dot(value, matrix[...], precision=HIGHEST, preferred_element_type=f32)
    image[...] = applied
    across = (((1,), (1,)), ((), ()))
    loads = value.shape[0]
    grams[:, :loads] = lax.dot_general(
        value, applied, across, precision=HIGHEST, preferred_element_type=f32
    )
    plus = jnp.concatenate([value[:, 256 * d + 128 : 256 * d + 256] for d in range(3)], axis=1)
    grams[:, loads:] = lax.dot_general(
        plus, plus, across, precision=HIGHEST, preferred_element_type=f32
    )
    send_faces(flags, image, outgoing)


def solve(table):
    size = table.shape[0]
    row = lax.broadcasted_iota(jnp.int32, table.shape, 0)
    for begin in range(0, size, 4):
        columns = [
            jnp.broadcast_to(table[:, k : k + 1], table.shape) for k in range(begin, begin + 4)
        ]
        for i in range(4):
            k = begin + i
            column = columns[i]
            inverse = 1.0 / column[k : k + 1]
            pivot = table[k : k + 1] * inverse
            table = jnp.where(row == k, pivot, table - column * pivot)
            for j in range(i + 1, 4):
                pivot = columns[j][k : k + 1] * inverse
                columns[j] = jnp.where(row == k, pivot, columns[j] - column * pivot)
    return table[:, size:]


def final_kernel(flags, grams, multipliers, residual, field, image, *refs):
    arrived, (new_multipliers, new_residual) = refs[:6], refs[6:]
    step = solve(grams[...]).T
    change = jnp.dot(step, field[...], precision=HIGHEST, preferred_element_type=f32)
    for f in range(6):
        lanes = slice(128 * f, 128 * (f + 1))
        new_multipliers[f] = multipliers[:, lanes] + change[:, lanes]
        applied = assembled(flags, image, arrived, f)
        new_residual[f] = residual[:, lanes] - jnp.dot(
            step, applied, precision=HIGHEST, preferred_element_type=f32
        )


def call(kernel, outs, *args, stored=None, **options):
    flags = pl.BlockSpec(memory_space=pltpu.SMEM)
    block = pl.BlockSpec(memory_space=pltpu.VMEM)
    return pl.pallas_call(
        kernel,
        out_shape=[jax.ShapeDtypeStruct(shape, kind) for shape, kind in outs],
        in_specs=[flags]
        + [pl.BlockSpec(memory_space=pltpu.HBM) if i == stored else block for i in range(1, len(args))],
        out_specs=[block] * len(outs),
        compiler_params=pltpu.CompilerParams(vmem_limit_bytes=24 << 20),
        **options,
    )(*args)


def body(compliance, rigid_modes, coarse_inverse, coarse_rhs, dual_rhs):
    face, loads = dual_rhs.shape[-1], dual_rhs.shape[-2]
    modes = rigid_modes.shape[3]
    long, plane = lax.axis_size("gx"), lax.axis_size(PLANE)
    parts = long * plane
    matrix = pltpu.with_memory_space_constraint(compliance[0, 0, 0], pltpu.HBM)
    traces = rigid_modes[0, 0, 0].transpose(1, 2, 0, 3).reshape(6, modes, face)
    gaps = dual_rhs[0, 0, 0].reshape(6, loads, face)
    right_side = coarse_rhs[0, 0, 0].reshape(modes, 1, loads)
    where = [lax.axis_index(axis) for axis in AXES]
    flags = jnp.stack([w % 2 for w in where] + [jnp.minimum(w, 1) for w in where]).astype(jnp.int32)
    wide, faces = ((loads, 6 * face), f32), ((6, loads, face), f32)
    held = [pltpu.VMEM(matrix.shape, f32), pltpu.SemaphoreType.DMA]
    packs = ((8, modes * parts + face), f32)

    row = ((long, modes // 2 + 1, 2 * loads), bf16)

    def along(rows):
        return lax.all_to_all(rows, "gx", 0, 0, tiled=True)

    def across(column):
        column = call(
            widen_kernel, [((plane, long, modes * loads), bf16)], flags, column, name="widen"
        )[0]
        return lax.all_to_all(column, PLANE, 0, 0, tiled=True).reshape(parts, modes * loads)

    column = along(call(modes_kernel, [row], flags, right_side, name="modes")[0])
    packed = call(
        functools.partial(prepare, modes, long, plane),
        [packs] * 6,
        flags,
        coarse_inverse,
        rigid_modes[0, 0, 0],
        scratch_shapes=[pltpu.VMEM((modes * parts, 8), f32)],
        name="prepare_rows",
    )
    in_plane = swap(packed[2:], PLANE)
    arrived = swap(packed[:2], AXES[:1])
    arrived += [pltpu.with_memory_space_constraint(a, pltpu.HBM) for a in in_plane]
    stacked = across(column)
    pieces, spread = call(
        functools.partial(build, modes, parts),
        [((modes // 2, 3 * 14 * 8, parts), bf16), ((7 * 8, 6 * face), f32)],
        flags,
        traces,
        packed[0],
        *arrived,
        name="build_rows",
    )

    multipliers, image, *outgoing = call(
        start_kernel,
        [wide, wide] + [((loads, face), f32)] * 6,
        flags,
        stacked,
        pieces,
        spread,
        matrix,
        stored=4,
        scratch_shapes=held,
        name="start_fields",
    )
    residual, sums = call(
        residual_kernel,
        [wide, row],
        flags,
        gaps,
        traces,
        image,
        *swap(outgoing),
        name="residual",
    )
    projected, image, grams, *outgoing = call(
        project_kernel,
        [wide, wide, ((loads, 2 * loads), f32)] + [((loads, face), f32)] * 6,
        flags,
        across(along(sums)),
        pieces,
        spread,
        matrix,
        residual,
        stored=4,
        scratch_shapes=held,
        name="project",
    )
    grams = lax.all_to_all(
        grams.reshape(plane, loads // plane, 2 * loads), PLANE, 0, 0, tiled=True
    ).sum(0)
    grams = to_all(grams, "gx").sum(0)
    grams = to_all(grams, PLANE).reshape(loads, 2 * loads)
    arrived = swap(outgoing)
    outputs = call(
        final_kernel,
        [faces, faces],
        flags,
        grams,
        multipliers,
        residual,
        projected,
        image,
        *arrived,
        name="final_update",
    )
    return tuple(out.reshape(1, 1, 1, 3, 2, loads, face) for out in outputs)


def solution(mesh):
    placed = (
        P("gx", "gy", "gz", None, None),
        P("gx", "gy", "gz", None, None, None, None),
        P(AXES, None),
        P("gx", "gy", "gz", None, None),
        P("gx", "gy", "gz", None, None, None, None),
    )

    return jax.shard_map(
        body,
        mesh=mesh,
        in_specs=placed,
        out_specs=(
            P("gx", "gy", "gz", None, None, None, None),
            P("gx", "gy", "gz", None, None, None, None),
        ),
        check_vma=False,
    )
```

```python
import functools

import jax
import jax.numpy as jnp
from jax import lax
from jax.experimental import pallas as pl
from jax.experimental.pallas import tpu as pltpu
from jax.sharding import PartitionSpec as P


HIGHEST = lax.Precision.HIGHEST
AXES = ("gx", "gy", "gz")
PLANE = ("gy", "gz")
bf16 = jnp.bfloat16
f32 = jnp.float32


def to_all(block, axis):
    return lax.all_to_all(
        jnp.broadcast_to(block[None], (lax.axis_size(axis),) + block.shape), axis, 0, 0, tiled=True
    )


def swap(outgoing, axes=AXES):
    arrived = []
    for d, axis in enumerate(axes):
        size = lax.axis_size(axis)
        even = [(i, i ^ 1) for i in range(size)]
        odd = [(i, i + 1 if i % 2 else i - 1) for i in range(1, size - 1)]
        arrived.append(lax.ppermute(outgoing[2 * d], axis, even))
        arrived.append(lax.ppermute(outgoing[2 * d + 1], axis, odd))
    return arrived


def pick(is_even, f, pair):
    even, odd = pair
    first, second = (odd, even) if f % 2 == 0 else (even, odd)
    return jnp.where(is_even, first, second)


def prepare(modes, long, plane, flags, rows, traces, *packed):
    turned = packed[-1]
    packed = packed[:-1]
    parts = long * plane
    blank = jnp.zeros((8 - modes, 128), f32)
    for b in range(modes * parts // 128):
        block = jnp.concatenate([rows[:, 128 * b : 128 * (b + 1)], blank], axis=0)
        turned[128 * b : 128 * (b + 1), :] = block.T
    group = 128 // long
    for j in range(modes):
        for b in range(parts // 128):
            strips = [
                turned[pl.ds((group * b + i) * modes + j, long, stride=plane * modes), :]
                for i in range(group)
            ]
            block = jnp.concatenate(strips, axis=0).T
            begin = j * parts + 128 * b
            for out in packed:
                out[:, begin : begin + 128] = block
    for d in range(3):
        is_even = flags[d] == 0
        minus = jnp.concatenate([traces[:, d, 0, :], blank], axis=0)
        plus = jnp.concatenate([traces[:, d, 1, :], blank], axis=0)
        packed[2 * d][:, modes * parts :] = jnp.where(is_even, plus, minus)
        packed[2 * d + 1][:, modes * parts :] = jnp.where(is_even, minus, plus)


def build(modes, parts, flags, traces, own, *refs):
    arrived, (pieces, spread) = refs[:6], refs[6:]
    width = modes * parts
    height = 14 * 8
    evens = [flags[d] == 0 for d in range(3)]
    blank = jnp.zeros((8 - modes, 128), f32)

    def take(source, begin, size):
        if source == 0:
            return own[:, begin : begin + size]
        f = source - 1
        pair = [r[:, begin : begin + size] for r in arrived[2 * (f // 2) : 2 * (f // 2) + 2]]
        return pick(evens[f // 2], f, pair)

    for q in range(modes // 2):
        for t in range(7):
            blocks = []
            for g in (2 * t, 2 * t + 1):
                half, source = divmod(g, 7)
                blocks.append(take(source, (2 * q + half) * parts, parts))
            value = jnp.concatenate(blocks, axis=0)
            for piece in range(3):
                rounded = value.astype(bf16)
                pieces[q, piece * height + 16 * t : piece * height + 16 * (t + 1), :] = rounded
                value = value - rounded.astype(f32)
    spread[...] = jnp.zeros_like(spread)
    for f in range(6):
        lanes = slice(128 * f, 128 * (f + 1))
        mine = jnp.concatenate([traces[f], blank], axis=0)
        other = -take(f + 1, width, 128)
        if f % 2 == 0:
            inside = flags[3 + f // 2] > 0
            mine = jnp.where(inside, mine, 0.0)
            other = jnp.where(inside, other, 0.0)
        spread[0:8, lanes] = mine
        spread[8 * (f + 1) : 8 * (f + 2), lanes] = other


def coarse(stacked, pieces, spread):
    lanes = stacked.shape[1] // pieces.shape[0]
    total = jnp.zeros((pieces.shape[1], lanes), f32)
    for q in range(pieces.shape[0]):
        total = total + jnp.dot(
            pieces[q], stacked[:, lanes * q : lanes * (q + 1)], preferred_element_type=f32
        )
    height = pieces.shape[1] // 3
    total = total[:height] + (total[height : 2 * height] + total[2 * height :])
    weights = total[: height // 2, : lanes // 2] + total[height // 2 :, lanes // 2 :]
    return jnp.dot(weights.T, spread[...], precision=HIGHEST, preferred_element_type=f32)


def send_faces(flags, wide, outgoing):
    for d in range(3):
        minus = wide[:, 256 * d : 256 * d + 128]
        plus = wide[:, 256 * d + 128 : 256 * d + 256]
        outgoing[2 * d][...] = jnp.where(flags[d] == 0, plus, minus)
        outgoing[2 * d + 1][...] = jnp.where(flags[d] == 0, minus, plus)


def assembled(flags, wide, arrived, f):
    d = f // 2
    pair = (arrived[2 * d][...], arrived[2 * d + 1][...])
    value = wide[:, 128 * f : 128 * (f + 1)] - pick(flags[d] == 0, f, pair)
    return jnp.where(flags[3 + d] > 0, value, 0.0) if f % 2 == 0 else value


def as_rows(sums, out):
    modes, loads = sums.shape
    rows = [jnp.concatenate([sums[m : m + 1], sums[m + 1 : m + 2]], axis=1) for m in range(0, modes, 2)]
    rows = jnp.concatenate(rows + [jnp.zeros((1, 2 * loads), f32)], axis=0)
    out[...] = jnp.broadcast_to(rows[None], out.shape).astype(bf16)


def modes_kernel(flags, right_side, out):
    as_rows(jnp.concatenate([right_side[m] for m in range(right_side.shape[0])], axis=0), out)


def widen_kernel(lead, flags, column, out):
    value = column[...].astype(f32)
    if lead:
        value = jnp.concatenate([value[-lead:], value[:-lead]], axis=0)
    wide = jnp.concatenate([value[:, q, :] for q in range(value.shape[1] - 1)], axis=1).astype(bf16)
    for p in range(out.shape[0]):
        out[p] = wide


def start_kernel(flags, stacked, pieces, spread, stored, field, image, *refs):
    outgoing, (matrix, arrival) = refs[:6], refs[6:]
    copy = pltpu.make_async_copy(stored, matrix, arrival)
    copy.start()
    value = coarse(stacked, pieces, spread)
    field[...] = value
    copy.wait()
    image[...] = jnp.dot(value, matrix[...], precision=HIGHEST, preferred_element_type=f32)
    send_faces(flags, image, outgoing)


def residual_kernel(flags, gaps, traces, image, *refs):
    arrived, (residual, sums) = refs[:6], refs[6:]
    total = 0.0
    for f in range(6):
        value = gaps[f] - assembled(flags, image, arrived, f)
        residual[:, 128 * f : 128 * (f + 1)] = value
        total = total + lax.dot_general(
            traces[f], value, (((1,), (1,)), ((), ())), precision=HIGHEST, preferred_element_type=f32
        )
    as_rows(total, sums)


def project_kernel(flags, stacked, pieces, spread, stored, residual, field, image, grams, *refs):
    outgoing, (matrix, arrival) = refs[:6], refs[6:]
    copy = pltpu.make_async_copy(stored, matrix, arrival)
    copy.start()
    value = residual[...] - coarse(stacked, pieces, spread)
    field[...] = value
    copy.wait()
    applied = jnp.dot(value, matrix[...], precision=HIGHEST, preferred_element_type=f32)
    image[...] = applied
    across = (((1,), (1,)), ((), ()))
    loads = value.shape[0]
    grams[:, :loads] = lax.dot_general(
        value, applied, across, precision=HIGHEST, preferred_element_type=f32
    )
    plus = jnp.concatenate([value[:, 256 * d + 128 : 256 * d + 256] for d in range(3)], axis=1)
    grams[:, loads:] = lax.dot_general(
        plus, plus, across, precision=HIGHEST, preferred_element_type=f32
    )
    send_faces(flags, image, outgoing)


def solve(table):
    size = table.shape[0]
    row = lax.broadcasted_iota(jnp.int32, table.shape, 0)
    for begin in range(0, size, 4):
        columns = [
            jnp.broadcast_to(table[:, k : k + 1], table.shape) for k in range(begin, begin + 4)
        ]
        for i in range(4):
            k = begin + i
            column = columns[i]
            inverse = 1.0 / column[k : k + 1]
            pivot = table[k : k + 1] * inverse
            table = jnp.where(row == k, pivot, table - column * pivot)
            for j in range(i + 1, 4):
                pivot = columns[j][k : k + 1] * inverse
                columns[j] = jnp.where(row == k, pivot, columns[j] - column * pivot)
    return table[:, size:]


def final_kernel(flags, grams, multipliers, residual, field, image, *refs):
    arrived, (new_multipliers, new_residual) = refs[:6], refs[6:]
    step = solve(grams[...]).T
    change = jnp.dot(step, field[...], precision=HIGHEST, preferred_element_type=f32)
    for f in range(6):
        lanes = slice(128 * f, 128 * (f + 1))
        new_multipliers[f] = multipliers[:, lanes] + change[:, lanes]
        applied = assembled(flags, image, arrived, f)
        new_residual[f] = residual[:, lanes] - jnp.dot(
            step, applied, precision=HIGHEST, preferred_element_type=f32
        )


def call(kernel, outs, *args, stored=None, **options):
    flags = pl.BlockSpec(memory_space=pltpu.SMEM)
    block = pl.BlockSpec(memory_space=pltpu.VMEM)
    return pl.pallas_call(
        kernel,
        out_shape=[jax.ShapeDtypeStruct(shape, kind) for shape, kind in outs],
        in_specs=[flags]
        + [pl.BlockSpec(memory_space=pltpu.HBM) if i == stored else block for i in range(1, len(args))],
        out_specs=[block] * len(outs),
        compiler_params=pltpu.CompilerParams(vmem_limit_bytes=24 << 20),
        **options,
    )(*args)


def body(compliance, rigid_modes, coarse_inverse, coarse_rhs, dual_rhs):
    face, loads = dual_rhs.shape[-1], dual_rhs.shape[-2]
    modes = rigid_modes.shape[3]
    long, plane = lax.axis_size("gx"), lax.axis_size(PLANE)
    parts = long * plane
    matrix = pltpu.with_memory_space_constraint(compliance[0, 0, 0], pltpu.HBM)
    traces = rigid_modes[0, 0, 0].transpose(1, 2, 0, 3).reshape(6, modes, face)
    gaps = dual_rhs[0, 0, 0].reshape(6, loads, face)
    right_side = coarse_rhs[0, 0, 0].reshape(modes, 1, loads)
    where = [lax.axis_index(axis) for axis in AXES]
    flags = jnp.stack([w % 2 for w in where] + [jnp.minimum(w, 1) for w in where]).astype(jnp.int32)
    wide, faces = ((loads, 6 * face), f32), ((6, loads, face), f32)
    held = [pltpu.VMEM(matrix.shape, f32), pltpu.SemaphoreType.DMA]
    packs = ((8, modes * parts + face), f32)

    row = ((long, modes // 2 + 1, 2 * loads), bf16)

    def along(rows, lead=0):
        group = [[(i + lead) % long for i in range(long)]] if lead else None
        return lax.all_to_all(rows, "gx", 0, 0, axis_index_groups=group, tiled=True)

    def across(column, lead=0):
        column = call(
            functools.partial(widen_kernel, lead),
            [((plane, long, modes * loads), bf16)],
            flags,
            column,
            name="widen",
        )[0]
        return lax.all_to_all(column, PLANE, 0, 0, tiled=True).reshape(parts, modes * loads)

    middle = long // 2
    column = along(call(modes_kernel, [row], flags, right_side, name="modes")[0], middle)
    packed = call(
        functools.partial(prepare, modes, long, plane),
        [packs] * 6,
        flags,
        coarse_inverse,
        rigid_modes[0, 0, 0],
        scratch_shapes=[pltpu.VMEM((modes * parts, 8), f32)],
        name="prepare_rows",
    )
    in_plane = swap(packed[2:], PLANE)
    arrived = swap(packed[:2], AXES[:1])
    arrived += [pltpu.with_memory_space_constraint(a, pltpu.HBM) for a in in_plane]
    stacked = across(column, middle)
    pieces, spread = call(
        functools.partial(build, modes, parts),
        [((modes // 2, 3 * 14 * 8, parts), bf16), ((7 * 8, 6 * face), f32)],
        flags,
        traces,
        packed[0],
        *arrived,
        name="build_rows",
    )

    multipliers, image, *outgoing = call(
        start_kernel,
        [wide, wide] + [((loads, face), f32)] * 6,
        flags,
        stacked,
        pieces,
        spread,
        matrix,
        stored=4,
        scratch_shapes=held,
        name="start_fields",
    )
    residual, sums = call(
        residual_kernel,
        [wide, row],
        flags,
        gaps,
        traces,
        image,
        *swap(outgoing),
        name="residual",
    )
    projected, image, grams, *outgoing = call(
        project_kernel,
        [wide, wide, ((loads, 2 * loads), f32)] + [((loads, face), f32)] * 6,
        flags,
        across(along(sums)),
        pieces,
        spread,
        matrix,
        residual,
        stored=4,
        scratch_shapes=held,
        name="project",
    )
    grams = lax.all_to_all(
        grams.reshape(plane, loads // plane, 2 * loads), PLANE, 0, 0, tiled=True
    ).sum(0)
    grams = to_all(grams, "gx").sum(0)
    grams = to_all(grams, PLANE).reshape(loads, 2 * loads)
    arrived = swap(outgoing)
    outputs = call(
        final_kernel,
        [faces, faces],
        flags,
        grams,
        multipliers,
        residual,
        projected,
        image,
        *arrived,
        name="final_update",
    )
    return tuple(out.reshape(1, 1, 1, 3, 2, loads, face) for out in outputs)


def solution(mesh):
    placed = (
        P("gx", "gy", "gz", None, None),
        P("gx", "gy", "gz", None, None, None, None),
        P(AXES, None),
        P("gx", "gy", "gz", None, None),
        P("gx", "gy", "gz", None, None, None, None),
    )

    return jax.shard_map(
        body,
        mesh=mesh,
        in_specs=placed,
        out_specs=(
            P("gx", "gy", "gz", None, None, None, None),
            P("gx", "gy", "gz", None, None, None, None),
        ),
        check_vma=False,
    )
```
